256 devices in a mesh: dp: 32 (over z, x), ctx: 8 (over y, core).
Axes of the slice: x: 4, y: 4, z: 8, core: 2. Of those that a mesh axis runs over, the one named last changes fastest.
Arguments:
- tokens: bfloat16 [32768, 8192], P(('dp', 'ctx')), may hold values from -24 to 24
- qkv: bfloat16 [32768, 1280], P(('dp', 'ctx')), may hold values from -8 to 8
- grad_out: bfloat16 [32768, 1024], P(('dp', 'ctx')), may hold values from -6 to 6
- span_order: int32 [32, 16], P('dp'), may hold values from 0 to 15, each once within a row
Outputs:
- grad_weight: float32 [8192, 1280], P(('dp', 'ctx'))
The draws below stay inside these ranges and needn't reach their ends.
Inputs may be any that keep to these rules, and one draw needn't show every extreme that they name: Each row of span_order is a permutation of 0 to 15.
All inputs are finite; a program needn't handle non-finite values.
Results may differ from the reference program's by a relative error of at most 0.023.
Values may be sent and summed in bfloat16 or wider, within the bound.
A program may use at most 64 MiB of HBM per device.

```python
import math
import jax
import jax.numpy as jnp
from jax import lax

D = 8192
HEADS = 8
HD = 128
T_DEV = 128
SPAN = 64
SPANS = 16
SEQ = 1024
SEQS = 32
TOKENS = 32768
QW = 1024
PW = 1280
N_CTX = 8


def draw_qkv(key, part):
    first_key = jax.random.fold_in(jax.random.fold_in(key, 11), 0)
    base = jnp.clip(jax.random.normal(first_key, (TOKENS, PW), jnp.float32), -6.0, 6.0)
    return base.astype(jnp.bfloat16)


def spiked(values, rng, source, target, shards_of, factor):
    owner, partner = [(jnp.arange(values.shape[position]) // (values.shape[position] // shards_of)).reshape([-1 if axis == position else 1 for axis in range(values.ndim)]) for position in (source, target)]
    chosen = jax.random.permutation(rng, shards_of)[partner]
    strong = (owner == chosen) | (owner == (partner + shards_of // 2) % shards_of)
    return jnp.where(strong, factor * values, values)


def block_levels(own_key, dims, cuts, smallest, top_value):
    loudness = 1.0
    for position, blocks in cuts:
        heights = jax.random.uniform(jax.random.fold_in(jax.random.fold_in(own_key, 6), position), (blocks,), jnp.float32, smallest / len(cuts), top_value / len(cuts))
        loudness = loudness * jnp.repeat(jnp.exp(heights), dims[position] // blocks).reshape((-1,) + (1,) * (len(dims) - 1 - position))
    return loudness


def centred(key, extent, scale, reach, cuts=(), kind=jnp.bfloat16):
    entries = scale * jax.random.normal(key, extent, jnp.float32)
    if cuts:
        entries = entries * block_levels(key, extent, cuts, -0.22, 0.18)
    return jnp.clip(entries, -reach, reach).astype(kind)


def bell_draw_with(own_key, dims, deviation, reach, cuts, heavy, held_as=jnp.bfloat16):
    array = deviation * jax.random.normal(own_key, dims, jnp.float32)
    if cuts:
        array = array * block_levels(own_key, dims, cuts, -0.22, 0.18)
    return jnp.clip(spiked(array, jax.random.fold_in(own_key, 3), *heavy), -reach, reach).astype(held_as)


def setup_inputs(seed: int = 0) -> dict:
    arg_keys = jax.random.split(jax.random.key(seed), 5)
    return {
        "tokens": bell_draw_with(arg_keys[0], (TOKENS, D), 1.0, 24.0, ((0, 256),), (0, 1, 256, 6.0)),
        "qkv": draw_qkv(jax.random.fold_in(arg_keys[4], 71), 0),
        "grad_out": centred(arg_keys[2], (TOKENS, QW), 1.0, 6.0, ((0, 256),)),
        "span_order": jax.vmap(lambda own: jax.random.permutation(own, SPANS))(jax.random.split(arg_keys[3], SEQS)).reshape((SEQS, SPANS)).astype(jnp.int32),
    }


theta_base = 500000.0

def angles(positions, width):
    half = width // 2
    freq = jnp.exp(-(jnp.arange(half, dtype=jnp.float32) * 2.0 / width) * jnp.log(jnp.float32(theta_base)))
    turn = positions.astype(jnp.float32)[:, None] * freq[None, :]
    return (jnp.cos(turn), jnp.sin(turn))

def rotate(values, cosine, sine):
    half = values.shape[-1] // 2
    first = values[..., :half]
    second = values[..., half:]
    return jnp.concatenate([first * cosine - second * sine, second * cosine + first * sine], axis=-1)

def rotate_back(grads, cosine, sine):
    half = grads.shape[-1] // 2
    first = grads[..., :half]
    second = grads[..., half:]
    return jnp.concatenate([first * cosine + second * sine, second * cosine - first * sine], axis=-1)

def sequence_grads(proj_b, upstream_b, order):
    scale = 1.0 / math.sqrt(HD)
    offsets = jnp.arange(SPAN, dtype=jnp.int32)
    key_pos = (order[:, None] * SPAN + offsets[None, :]).reshape(-1).astype(jnp.int32)
    cosine, sine = angles(key_pos, HD)
    proj = proj_b.astype(jnp.float32)
    rows = HEADS * SEQ
    queries = proj[:, :QW].reshape(SEQ, HEADS, HD).transpose(1, 0, 2)
    queries = rotate(queries, cosine, sine).astype(jnp.bfloat16).reshape(rows, HD)
    keys = rotate(proj[:, QW:QW + HD], cosine, sine).astype(jnp.bfloat16)
    values = proj_b[:, QW + HD:]
    query_pos = jnp.tile(key_pos, HEADS)
    raw = jnp.dot(queries, keys.T, preferred_element_type=jnp.float32) * scale
    scores = jnp.where(key_pos[None, :] <= query_pos[:, None], raw, -jnp.inf)
    peak = lax.optimization_barrier(jnp.max(scores, axis=1, keepdims=True))
    expo = jnp.exp(scores - peak)
    probs = expo / lax.optimization_barrier(jnp.sum(expo, axis=1, keepdims=True))
    probs_b = probs.astype(jnp.bfloat16)
    output = jnp.dot(probs_b, values, preferred_element_type=jnp.float32)
    upstream = upstream_b.reshape(SEQ, HEADS, HD).transpose(1, 0, 2).reshape(rows, HD)
    delta = lax.optimization_barrier(jnp.sum(upstream.astype(jnp.float32) * output, axis=1))
    dprobs = jnp.dot(upstream, values.T, preferred_element_type=jnp.float32)
    dscores = (probs * (dprobs - delta[:, None])).astype(jnp.bfloat16)
    dq = jnp.dot(dscores, keys, preferred_element_type=jnp.float32) * scale
    dk = jnp.dot(dscores.T, queries, preferred_element_type=jnp.float32) * scale
    dv = jnp.dot(probs_b.T, upstream, preferred_element_type=jnp.float32)
    dq_rows = rotate_back(dq.reshape(HEADS, SEQ, HD), cosine, sine).transpose(1, 0, 2).reshape(SEQ, QW)
    dk_rows = rotate_back(dk, cosine, sine)
    return jnp.concatenate([dq_rows, dk_rows, dv], axis=1).astype(jnp.bfloat16)

def reference(tokens, qkv, grad_out, span_order):
    seq_tokens = tokens.reshape(SEQS, SEQ, D)
    seq_proj = qkv.reshape(SEQS, SEQ, PW)
    seq_up = grad_out.reshape(SEQS, SEQ, QW)

    def one(total, item):
        inputs, proj_b, upstream_b, order = item
        grads_qkv = sequence_grads(proj_b, upstream_b, order)
        input_parts = inputs.reshape(N_CTX, T_DEV, D)
        grad_parts = grads_qkv.reshape(N_CTX, T_DEV, PW)

        def add(acc, pair):
            part = lax.dot_general(pair[0], pair[1], (((0,), (0,)), ((), ())), preferred_element_type=jnp.float32)
            rounded = lax.optimization_barrier(part.astype(jnp.bfloat16))
            return (acc + rounded.astype(jnp.float32), None)
        total, _ = lax.scan(add, total, (input_parts, grad_parts))
        return (total, None)
    start = jnp.zeros((D, PW), jnp.float32)
    result, _ = lax.scan(one, start, (seq_tokens, seq_proj, seq_up, span_order.astype(jnp.int32)))
    return result
```

```python
import functools
import math

import jax
import jax.numpy as jnp
from jax import lax
from jax.experimental import pallas as pl
from jax.experimental.pallas import tpu as pltpu
from jax.sharding import PartitionSpec as P

HEADS = 8
HD = 128
TDEV = 128
SEQ = 1024
QW = HEADS * HD
NX = 4
NZ = 8
SPAN = 64
SPANS = 16
LOG_BASE = math.log(500000.0)
SCALE = 1.0 / math.sqrt(HD)
LOG2E = 1.4426950408889634
MESH = pl.DeviceIdType.MESH
BF = jnp.bfloat16
F32 = jnp.float32
CHUNKS = ((0, 512), (512, 512), (1024, 256))
LAGS = (0, 0, 1)


def kernel(
    tok_h, qkv_h, go_h, span_s, out_ref,
    tokv, qkvv, gov, q_s, g_s, kv, bias, cos_s, sin_s, dkt, dvt, dsend, drecv,
    tr, at, bq_own, bk_own, bq, bk, y1s, y1r, y2s, y2r, cacc, zs, zr,
    lsem, kvs, kvr, asnd, arcv, dss, dsr, bs, br, cs, cr,
):
    dp = lax.axis_index("dp")
    ctx = lax.axis_index("ctx")
    z = dp // NX
    x = dp % NX
    y = ctx // 2
    c = ctx % 2

    def dev(zz, xx, yy, cc):
        return (zz * NX + xx, yy * 2 + cc)

    def rcopy(src, dst, ssem, rsem, to):
        return pltpu.make_async_remote_copy(
            src_ref=src, dst_ref=dst, send_sem=ssem, recv_sem=rsem,
            device_id=to, device_id_type=MESH,
        )

    pending = []

    def send(src, dst, ssem, rsem, to):
        copy = rcopy(src, dst, ssem, rsem, to)
        copy.start()
        pending.append(copy)

    partner = dev(z, x, y, 1 - c)

    def got(dst, sem):
        rcopy(dst, dst, kvs.at[0], sem, partner).wait_recv()

    loads = [
        pltpu.make_async_copy(qkv_h, qkvv, lsem.at[0]),
        pltpu.make_async_copy(go_h, gov, lsem.at[1]),
        pltpu.make_async_copy(tok_h, tokv, lsem.at[2]),
    ]
    for load in loads:
        load.start()

    barrier = pltpu.get_barrier_semaphore()
    peers = [partner]
    for off in range(1, NX):
        for cc in range(2):
            peers.append(dev(z, x, (y + off) % NX, cc))
            peers.append(dev(z, (x + off) % NX, y, cc))
    peers.append(dev((z + 1) % NZ, x, y, c))
    peers.append(dev((z + NZ - 1) % NZ, x, y, c))
    for peer in peers:
        pl.semaphore_signal(barrier, inc=1, device_id=peer, device_id_type=MESH)

    rows = lax.broadcasted_iota(jnp.int32, (TDEV, HD), 0)
    lanes = lax.broadcasted_iota(jnp.int32, (TDEV, HD), 1)
    first = span_s[0, 2 * ctx]
    second = span_s[0, 2 * ctx + 1]
    pos = jnp.where(rows < SPAN, first * SPAN + rows, second * SPAN + rows - SPAN)
    half = (lanes % (HD // 2)).astype(F32)
    freq = jnp.exp(half * (-2.0 / HD) * jnp.float32(LOG_BASE))
    angle = pos.astype(F32) * freq
    cosine = jnp.cos(angle)
    sine = jnp.sin(angle)
    sine = jnp.where(lanes < HD // 2, -sine, sine)
    cos_s[...] = cosine
    sin_s[...] = sine

    def rot(a):
        return a * cosine + pltpu.roll(a, HD // 2, 1) * sine

    loads[0].wait()
    kv_rows = pl.ds(pl.multiple_of(ctx * TDEV, TDEV), TDEV)
    kv[kv_rows, :HD] = rot(qkvv[:, QW:QW + HD].astype(F32)).astype(BF)
    kv[kv_rows, HD:] = qkvv[:, QW + HD:]

    pl.semaphore_wait(barrier, len(peers))

    own_kv = kv.at[kv_rows, :]
    for off in range(1, NX):
        send(own_kv, own_kv, kvs.at[off - 1], kvr.at[off - 1], dev(z, x, (y + off) % NX, c))
    send(own_kv, own_kv, kvs.at[3], kvr.at[3], partner)

    loads[2].wait()

    def turn(zz, carry):
        for xx in range(NX):
            block = tokv[:, pl.ds(pl.multiple_of(zz * 1024 + xx * 256, 256), 256)]
            flip = block.T
            for yy in range(NX):
                at_row = pl.multiple_of(zz * 32, 32)
                tr[0, xx, pl.ds(yy * 256 + at_row, 32), :] = flip[yy * 64:yy * 64 + 32]
                tr[1, yy, pl.ds(xx * 256 + at_row, 32), :] = flip[yy * 64 + 32:yy * 64 + 64]
        return carry

    lax.fori_loop(0, NZ, turn, 0)

    def slot(m):
        return pl.ds(pl.multiple_of(m * TDEV, TDEV), TDEV)

    gpos = x * (1 - c) + y * c
    opos = y * (1 - c) + x * c
    mine = slot(gpos * 2 + c)
    for off in (2, 1, 3):
        to_x = (x + off) % NX
        to_y = (y + off) % NX
        send(tr.at[0, to_x], at.at[:, slot(x * 2 + c)],
             asnd.at[off - 1], arcv.at[(off - 1) * 2 + c], dev(z, to_x, y, 0))
        send(tr.at[1, to_y], at.at[:, slot(y * 2 + c)],
             asnd.at[off + 2], arcv.at[(off - 1) * 2 + c], dev(z, x, to_y, 1))
    send(tr.at[1 - c, opos], at.at[:, slot(opos * 2 + c)], asnd.at[6], arcv.at[6], partner)
    own_a = pltpu.make_async_copy(tr.at[c, gpos], at.at[:, mine], lsem.at[3])
    own_a.start()

    for h in range(HEADS):
        q_s[h * TDEV:(h + 1) * TDEV, :] = rot(
            qkvv[:, h * HD:(h + 1) * HD].astype(F32)).astype(BF)
    loads[1].wait()
    for h in range(HEADS):
        g_s[h * TDEV:(h + 1) * TDEV, :] = gov[:, h * HD:(h + 1) * HD]
    key = lax.broadcasted_iota(jnp.int32, (1, SEQ), 1)
    key_span = key // SPAN
    key_pos = key % SPAN
    for i in range(SPANS):
        key_pos = key_pos + jnp.where(key_span == i, span_s[0, i] * SPAN, 0)
    masked = jnp.where(key_pos <= pos[:, :1], jnp.float32(0.0), jnp.float32(-1e30))
    bias[:TDEV, :] = masked
    bias[TDEV:, :] = masked
    dkt[...] = jnp.zeros_like(dkt)
    dvt[...] = jnp.zeros_like(dvt)

    for off in (1, 3, 2):
        rows_in = slot(((y + NX - off) % NX) * 2 + c)
        got(kv.at[rows_in, :], kvr.at[off - 1])
        send(kv.at[rows_in, :], kv.at[rows_in, :], kvs.at[3 + off], kvr.at[3 + off], partner)
    got(own_kv, kvr.at[3])
    for off in (1, 3, 2):
        got(own_kv, kvr.at[3 + off])

    def heads(i, carry):
        two = pl.ds(pl.multiple_of(i * 2 * TDEV, 2 * TDEV), 2 * TDEV)
        q2 = q_s[two, :]
        g2 = g_s[two, :]
        keys = kv[:, :HD]
        values = kv[:, HD:]
        s = lax.dot_general(q2, keys, (((1,), (1,)), ((), ())), preferred_element_type=F32)
        s = s * jnp.float32(SCALE * LOG2E) + bias[...]
        e = jnp.exp2(s - jnp.max(s, axis=1, keepdims=True))
        p = e * (1.0 / jnp.sum(e, axis=1, keepdims=True))
        pb = p.astype(BF)
        o = jnp.dot(pb, values, preferred_element_type=F32)
        delta = jnp.sum(g2.astype(F32) * o, axis=1, keepdims=True)
        dpr = lax.dot_general(g2, values, (((1,), (1,)), ((), ())), preferred_element_type=F32)
        ds = (p * (dpr - delta)).astype(BF)
        dq = jnp.dot(ds, keys, preferred_element_type=F32) * jnp.float32(SCALE)
        for j in range(2):
            g = dq[j * TDEV:(j + 1) * TDEV]
            back = g * cos_s[...] - pltpu.roll(g, HD // 2, 1) * sin_s[...]
            at_col = pl.multiple_of((2 * i + j) * HD, HD)
            bq_own[:, pl.ds(at_col, HD)] = back.astype(BF)
        dkt[...] += lax.dot_general(q2, ds, (((0,), (0,)), ((), ())), preferred_element_type=F32)
        dvt[...] += lax.dot_general(g2, pb, (((0,), (0,)), ((), ())), preferred_element_type=F32)
        return carry

    lax.fori_loop(0, HEADS // 2, heads, 0)

    for j in range(8):
        dsend[j, :HD, :] = dkt[:, j * TDEV:(j + 1) * TDEV].astype(BF)
        dsend[j, HD:, :] = dvt[:, j * TDEV:(j + 1) * TDEV].astype(BF)
    for off in range(1, 8):
        to = (ctx + off) % 8
        send(dsend.at[to], drecv.at[off - 1], dss.at[off - 1], dsr.at[off - 1], (dp, to))

    def spread(own, group, base, sem):
        for k, off in enumerate((1, NX - 1)):
            send(own, group.at[slot(x * 2 + c), :], bs.at[base + k],
                 br.at[base + 2 * k + c], dev(z, (x + off) % NX, y, 0))
            send(own, group.at[slot(y * 2 + c), :], bs.at[base + 2 + k],
                 br.at[base + 2 * k + c], dev(z, x, (y + off) % NX, 1))
        send(own, group.at[slot(opos * 2 + c), :], bs.at[base + 4], br.at[base + 6], partner)
        copy = pltpu.make_async_copy(own, group.at[mine, :], sem)
        copy.start()
        return copy

    def beside(step):
        return dev(z, (x + (1 - c) * step) % NX, (y + c * step) % NX, c)

    below = (gpos + NX - 1) % NX
    above = (gpos + 1) % NX

    def relay(group, base):
        up = group.at[slot(below * 2), :]
        got(up, br.at[base])
        send(up, up, bs.at[base + 5], br.at[base + 4], beside(1))
        down = group.at[slot(above * 2 + 1), :]
        got(down, br.at[base + 3])
        send(down, down, bs.at[base + 6], br.at[base + 5], beside(NX - 1))

    def rest(group, base, local):
        local.wait()
        for k in (1, 2, 4, 5, 6):
            got(group.at[mine, :], br.at[base + k])

    copy_q = spread(bq_own, bq, 0, lsem.at[4])
    relay(bq, 0)

    own_cols = pl.ds(pl.multiple_of(ctx * TDEV, TDEV), TDEV)
    for off in range(1, 8):
        got(drecv.at[off - 1], dsr.at[off - 1])
    dk = dkt[:, own_cols]
    dv = dvt[:, own_cols]
    for off in range(1, 8):
        dk = dk + drecv[off - 1, :HD, :].astype(F32)
        dv = dv + drecv[off - 1, HD:, :].astype(F32)
    dk = dk.T * jnp.float32(SCALE)
    bk_own[:, :HD] = (dk * cos_s[...] - pltpu.roll(dk, HD // 2, 1) * sin_s[...]).astype(BF)
    bk_own[:, HD:] = dv.T.astype(BF)
    copy_k = spread(bk_own, bk, 7, lsem.at[5])
    relay(bk, 7)

    own_a.wait()
    for k in range(7):
        got(at.at[:, mine], arcv.at[k])
    rest(bq, 0, copy_q)

    def across(step):
        return dev(z, (x + c * step) % NX, (y + (1 - c) * step) % NX, c)

    up_dev, down_dev = across(1), across(NX - 1)
    zup_dev, zdown_dev = dev((z + 1) % NZ, x, y, c), dev((z + NZ - 1) % NZ, x, y, c)

    def term(a, ch):
        first_col, width = CHUNKS[ch]
        lhs = at[pl.ds(pl.multiple_of(a * 256, 256), 256), :]
        if first_col < QW:
            rhs = bq[:, first_col:first_col + width]
        else:
            rhs = bk[:, first_col - QW:first_col - QW + width]
        return jnp.dot(lhs, rhs, preferred_element_type=F32)

    def zrows(zz):
        return pl.multiple_of(zz * 32, 32)

    def stage(ch, s):
        first_col, width = CHUNKS[ch]
        cols = slice(first_col, first_col + width)
        base = ch * 12
        if s == 0:
            y1s[:, cols] = term((opos + 2) % NX, ch).astype(BF)
            send(y1s.at[:128, cols], y1r.at[0, :, cols], cs.at[base], cr.at[base], up_dev)
            send(y1s.at[128:, cols], y1r.at[1, :, cols], cs.at[base + 1], cr.at[base + 1], down_dev)
        elif s == 1:
            t = term((opos + 1) % NX, ch)
            got(y1r.at[0, :, cols], cr.at[base])
            y2s[0, :128, cols] = (t[:128] + y1r[0, :, cols].astype(F32)).astype(BF)
            y2s[0, 128:, cols] = t[128:].astype(BF)
            send(y2s.at[0, :, cols], y2r.at[0, :, cols], cs.at[base + 2], cr.at[base + 2], up_dev)
            t = term((opos + NX - 1) % NX, ch)
            got(y1r.at[1, :, cols], cr.at[base + 1])
            y2s[1, :128, cols] = t[:128].astype(BF)
            y2s[1, 128:, cols] = (t[128:] + y1r[1, :, cols].astype(F32)).astype(BF)
            send(y2s.at[1, :, cols], y2r.at[1, :, cols], cs.at[base + 3], cr.at[base + 3], down_dev)
        elif s == 2:
            cacc[:, cols] = term(opos, ch)
            got(y2r.at[0, :, cols], cr.at[base + 2])
            got(y2r.at[1, :, cols], cr.at[base + 3])
            cacc[:, cols] += y2r[0, :, cols].astype(F32) + y2r[1, :, cols].astype(F32)
            far = zrows((z + 4) % NZ)
            zs[0, 0, :16, cols] = cacc[pl.ds(far, 16), cols].astype(BF)
            zs[0, 1, :16, cols] = cacc[pl.ds(far + 16, 16), cols].astype(BF)
            for d, to in enumerate((zup_dev, zdown_dev)):
                send(zs.at[0, d, :16, cols], zr.at[0, d, :16, cols],
                     cs.at[base + 4 + d], cr.at[base + 4 + d], to)
        elif s < 6:
            k = s - 2
            for d, to in enumerate((zup_dev, zdown_dev)):
                step = 4 - k
                blk = zrows((z + (step if d == 0 else NZ - step)) % NZ)
                sem = base + 4 + 2 * (k - 1) + d
                if k == 1:
                    got(zr.at[0, d, :16, cols], cr.at[sem])
                    low = cacc[pl.ds(blk, 16), cols]
                    high = cacc[pl.ds(blk + 16, 16), cols]
                    came = zr[0, d, :16, cols].astype(F32)
                    if d == 0:
                        low = low + came
                    else:
                        high = high + came
                    zs[k, d, :16, cols] = low.astype(BF)
                    zs[k, d, 16:, cols] = high.astype(BF)
                else:
                    got(zr.at[k - 1, d, :, cols], cr.at[sem])
                    zs[k, d, :, cols] = (
                        cacc[pl.ds(blk, 32), cols] + zr[k - 1, d, :, cols].astype(F32)
                    ).astype(BF)
                send(zs.at[k, d, :, cols], zr.at[k, d, :, cols],
                     cs.at[sem + 2], cr.at[sem + 2], to)
        else:
            for d in range(2):
                got(zr.at[3, d, :, cols], cr.at[base + 10 + d])
            out_ref[:, cols] = (
                cacc[pl.ds(zrows(z), 32), cols]
                + zr[3, 0, :, cols].astype(F32) + zr[3, 1, :, cols].astype(F32)
            )

    have_k = False
    for t in range(7 + max(LAGS)):
        for ch in range(len(CHUNKS)):
            s = t - LAGS[ch]
            if 0 <= s <= 6:
                if CHUNKS[ch][0] >= QW and not have_k:
                    rest(bk, 7, copy_k)
                    have_k = True
                stage(ch, s)

    for copy in pending:
        copy.wait_send()


def body(tokens, qkv, grad_out, span_order):
    n_c = 12 * len(CHUNKS)
    dma = pltpu.SemaphoreType.DMA
    v = pltpu.VMEM
    return pl.pallas_call(
        kernel,
        out_shape=jax.ShapeDtypeStruct((32, 1280), F32),
        in_specs=[pl.BlockSpec(memory_space=pl.ANY)] * 3
        + [pl.BlockSpec(memory_space=pltpu.SMEM)],
        out_specs=pl.BlockSpec(memory_space=pltpu.VMEM),
        scratch_shapes=[
            v((TDEV, 8192), BF), v((TDEV, 1280), BF), v((TDEV, QW), BF),
            v((SEQ, HD), BF), v((SEQ, HD), BF), v((SEQ, 2 * HD), BF),
            v((2 * TDEV, SEQ), F32), v((TDEV, HD), F32), v((TDEV, HD), F32),
            v((HD, SEQ), F32), v((HD, SEQ), F32),
            v((8, 2 * HD, TDEV), BF), v((7, 2 * HD, TDEV), BF),
            v((2, NX, 1024, TDEV), BF), v((1024, SEQ), BF),
            v((TDEV, QW), BF), v((TDEV, 256), BF), v((SEQ, QW), BF), v((SEQ, 256), BF),
            v((256, 1280), BF), v((2, 128, 1280), BF),
            v((2, 256, 1280), BF), v((2, 256, 1280), BF),
            v((256, 1280), F32), v((4, 2, 32, 1280), BF), v((4, 2, 32, 1280), BF),
            dma((6,)), dma((7,)), dma((7,)), dma((7,)), dma((7,)), dma((7,)), dma((7,)),
            dma((14,)), dma((14,)), dma((n_c,)), dma((n_c,)),
        ],
        compiler_params=pltpu.CompilerParams(collective_id=0, has_side_effects=True),
    )(tokens, qkv, grad_out, span_order)


def solution(mesh):
    return jax.shard_map(
        body,
        mesh=mesh,
        in_specs=(
            P(("dp", "ctx"), None),
            P(("dp", "ctx"), None),
            P(("dp", "ctx"), None),
            P("dp", None),
        ),
        out_specs=P(("dp", "ctx"), None),
        check_vma=False,
    )
```

```python
import functools
import math

import jax
import jax.numpy as jnp
from jax import lax
from jax.experimental import pallas as pl
from jax.experimental.pallas import tpu as pltpu
from jax.sharding import PartitionSpec as P

HEADS = 8
HD = 128
TDEV = 128
SEQ = 1024
QW = HEADS * HD
NX = 4
NZ = 8
SPAN = 64
SPANS = 16
LOG_BASE = math.log(500000.0)
SCALE = 1.0 / math.sqrt(HD)
LOG2E = 1.4426950408889634
MESH = pl.DeviceIdType.MESH
BF = jnp.bfloat16
F32 = jnp.float32
NQ = 2
PER = HEADS // NQ
QC = QW // NQ
WIDTHS = (QC,) * NQ + (2 * HD,)
STARTS = tuple(QC * i for i in range(NQ)) + (QW,)
NCH = NQ + 1
LAGS = (0, 1, 2)


def kernel(
    tok_h, qkv_h, go_h, span_s, out_ref,
    tokv, qkvv, gov, q_s, g_s, kv, bias, cos_s, sin_s, dkt, dvt, psend, precv, dsend, drecv,
    tr, at, bq_own, bk_own, bq, bk, y1s, y1r, y2s, y2r, cacc, zs, zr,
    lsem, kvs, kvr, asnd, arcv, dss, dsr, bs, br, cs, cr,
):
    dp = lax.axis_index("dp")
    ctx = lax.axis_index("ctx")
    z = dp // NX
    x = dp % NX
    y = ctx // 2
    c = ctx % 2

    def dev(zz, xx, yy, cc):
        return (zz * NX + xx, yy * 2 + cc)

    def rcopy(src, dst, ssem, rsem, to):
        return pltpu.make_async_remote_copy(
            src_ref=src, dst_ref=dst, send_sem=ssem, recv_sem=rsem,
            device_id=to, device_id_type=MESH,
        )

    pending = []

    def send(src, dst, ssem, rsem, to):
        copy = rcopy(src, dst, ssem, rsem, to)
        copy.start()
        pending.append(copy)

    partner = dev(z, x, y, 1 - c)

    def got(dst, sem):
        rcopy(dst, dst, kvs.at[0], sem, partner).wait_recv()

    loads = [
        pltpu.make_async_copy(qkv_h, qkvv, lsem.at[0]),
        pltpu.make_async_copy(go_h, gov, lsem.at[1]),
        pltpu.make_async_copy(tok_h, tokv, lsem.at[2]),
    ]
    for load in loads:
        load.start()

    barrier = pltpu.get_barrier_semaphore()
    peers = [dev((z + off) % NZ, x, y, c) for off in (1, 7, 2, 6)]
    for off in range(1, NX):
        for cc in range(2):
            peers.append(dev(z, x, (y + off) % NX, cc))
            peers.append(dev(z, (x + off) % NX, y, cc))
    peers.append(partner)
    for peer in peers:
        pl.semaphore_signal(barrier, inc=1, device_id=peer, device_id_type=MESH)

    rows = lax.broadcasted_iota(jnp.int32, (TDEV, HD), 0)
    lanes = lax.broadcasted_iota(jnp.int32, (TDEV, HD), 1)
    first = span_s[0, 2 * ctx]
    second = span_s[0, 2 * ctx + 1]
    pos = jnp.where(rows < SPAN, first * SPAN + rows, second * SPAN + rows - SPAN)
    half = (lanes % (HD // 2)).astype(F32)
    freq = jnp.exp(half * (-2.0 / HD) * jnp.float32(LOG_BASE))
    angle = pos.astype(F32) * freq
    cosine = jnp.cos(angle)
    sine = jnp.sin(angle)
    sine = jnp.where(lanes < HD // 2, -sine, sine)
    cos_s[...] = cosine
    sin_s[...] = sine

    def rot(a):
        return a * cosine + pltpu.roll(a, HD // 2, 1) * sine

    loads[0].wait()
    kv_rows = pl.ds(pl.multiple_of(ctx * TDEV, TDEV), TDEV)
    kv[kv_rows, :HD] = rot(qkvv[:, QW:QW + HD].astype(F32)).astype(BF)
    kv[kv_rows, HD:] = qkvv[:, QW + HD:]

    loads[2].wait()

    def turn(zz, carry):
        for xx in range(NX):
            block = tokv[:, pl.ds(pl.multiple_of(zz * 1024 + xx * 256, 256), 256)]
            flip = block.T
            for yy in range(NX):
                at_row = pl.multiple_of(zz * 32, 32)
                tr[0, xx, pl.ds(yy * 256 + at_row, 32), :] = flip[yy * 64:yy * 64 + 32]
                tr[1, yy, pl.ds(xx * 256 + at_row, 32), :] = flip[yy * 64 + 32:yy * 64 + 64]
        return carry

    lax.fori_loop(0, NZ, turn, 0)

    for h in range(HEADS):
        q_s[h * TDEV:(h + 1) * TDEV, :] = rot(
            qkvv[:, h * HD:(h + 1) * HD].astype(F32)).astype(BF)
    loads[1].wait()
    for h in range(HEADS):
        g_s[h * TDEV:(h + 1) * TDEV, :] = gov[:, h * HD:(h + 1) * HD]
    key = lax.broadcasted_iota(jnp.int32, (1, SEQ), 1)
    key_span = key // SPAN
    key_pos = key % SPAN
    for i in range(SPANS):
        key_pos = key_pos + jnp.where(key_span == i, span_s[0, i] * SPAN, 0)
    masked = jnp.where(key_pos <= pos[:, :1], jnp.float32(0.0), jnp.float32(-1e30))
    bias[:TDEV, :] = masked
    bias[TDEV:, :] = masked
    dkt[...] = jnp.zeros_like(dkt)
    dvt[...] = jnp.zeros_like(dvt)

    pl.semaphore_wait(barrier, len(peers))

    own_kv = kv.at[kv_rows, :]
    for off in range(1, NX):
        send(own_kv, own_kv, kvs.at[off - 1], kvr.at[off - 1], dev(z, x, (y + off) % NX, c))
    send(own_kv, own_kv, kvs.at[3], kvr.at[3], partner)

    def slot(m):
        return pl.ds(pl.multiple_of(m * TDEV, TDEV), TDEV)

    gpos = x * (1 - c) + y * c
    opos = y * (1 - c) + x * c
    mine = slot(gpos * 2 + c)
    for off in (2, 1, 3):
        to_x = (x + off) % NX
        to_y = (y + off) % NX
        send(tr.at[0, to_x], at.at[:, slot(x * 2 + c)],
             asnd.at[off - 1], arcv.at[(off - 1) * 2 + c], dev(z, to_x, y, 0))
        send(tr.at[1, to_y], at.at[:, slot(y * 2 + c)],
             asnd.at[off + 2], arcv.at[(off - 1) * 2 + c], dev(z, x, to_y, 1))
    send(tr.at[1 - c, opos], at.at[:, slot(opos * 2 + c)], asnd.at[6], arcv.at[6], partner)
    own_a = pltpu.make_async_copy(tr.at[c, gpos], at.at[:, mine], lsem.at[3])
    own_a.start()

    for off in (1, 3, 2):
        rows_in = slot(((y + NX - off) % NX) * 2 + c)
        got(kv.at[rows_in, :], kvr.at[off - 1])
        send(kv.at[rows_in, :], kv.at[rows_in, :], kvs.at[3 + off], kvr.at[3 + off], partner)
    got(own_kv, kvr.at[3])
    for off in (1, 3, 2):
        got(own_kv, kvr.at[3 + off])

    def heads(n, i, carry):
        pair = n * (PER // 2) + i
        two = pl.ds(pl.multiple_of(pair * 2 * TDEV, 2 * TDEV), 2 * TDEV)
        q2 = q_s[two, :]
        g2 = g_s[two, :]
        keys = kv[:, :HD]
        values = kv[:, HD:]
        s = lax.dot_general(q2, keys, (((1,), (1,)), ((), ())), preferred_element_type=F32)
        s = s * F32(SCALE * LOG2E) + bias[...]
        e = jnp.exp2(s - jnp.max(s, axis=1, keepdims=True))
        p = e * (1.0 / jnp.sum(e, axis=1, keepdims=True))
        pb = p.astype(BF)
        o = jnp.dot(pb, values, preferred_element_type=F32)
        delta = jnp.sum(g2.astype(F32) * o, axis=1, keepdims=True)
        dpr = lax.dot_general(g2, values, (((1,), (1,)), ((), ())), preferred_element_type=F32)
        ds = (p * (dpr - delta)).astype(BF)
        dq = jnp.dot(ds, keys, preferred_element_type=F32) * F32(SCALE)
        for j in range(2):
            g = dq[j * TDEV:(j + 1) * TDEV]
            back = g * cos_s[...] - pltpu.roll(g, HD // 2, 1) * sin_s[...]
            at_col = pl.multiple_of((2 * i + j) * HD, HD)
            bq_own[n, :, pl.ds(at_col, HD)] = back.astype(BF)
        dkt[...] += lax.dot_general(q2, ds, (((0,), (0,)), ((), ())), preferred_element_type=F32)
        dvt[...] += lax.dot_general(g2, pb, (((0,), (0,)), ((), ())), preferred_element_type=F32)
        return carry

    def own_of(ch):
        return bq_own.at[ch] if ch < NQ else bk_own

    def group_of(ch, where):
        return bq.at[ch, where, :] if ch < NQ else bk.at[where, :]

    local = []

    def spread(ch):
        own, base = own_of(ch), 7 * ch
        for k, off in enumerate((1, NX - 1)):
            send(own, group_of(ch, slot(x * 2 + c)), bs.at[base + k],
                 br.at[base + 2 * k + c], dev(z, (x + off) % NX, y, 0))
            send(own, group_of(ch, slot(y * 2 + c)), bs.at[base + 2 + k],
                 br.at[base + 2 * k + c], dev(z, x, (y + off) % NX, 1))
        send(own, group_of(ch, slot(opos * 2 + c)), bs.at[base + 4], br.at[base + 6], partner)
        copy = pltpu.make_async_copy(own, group_of(ch, mine), lsem.at[4 + ch])
        copy.start()
        local.append(copy)

    def beside(step):
        return dev(z, (x + (1 - c) * step) % NX, (y + c * step) % NX, c)

    below = (gpos + NX - 1) % NX
    above = (gpos + 1) % NX

    def relay(ch):
        base = 7 * ch
        up = group_of(ch, slot(below * 2))
        got(up, br.at[base])
        send(up, up, bs.at[base + 5], br.at[base + 4], beside(1))
        down = group_of(ch, slot(above * 2 + 1))
        got(down, br.at[base + 3])
        send(down, down, bs.at[base + 6], br.at[base + 5], beside(NX - 1))

    def rest(ch):
        local[ch].wait()
        for k in (1, 2, 4, 5, 6):
            got(group_of(ch, mine), br.at[7 * ch + k])

    for n in range(NQ):
        lax.fori_loop(0, PER // 2, functools.partial(heads, n), 0)
        if n < NQ - 1:
            spread(n)

    def part(ref, blk):
        return ref[:, pl.ds(pl.multiple_of(blk * TDEV, TDEV), TDEV)]

    for j in range(NX):
        psend[j, :HD, :] = part(dkt, 2 * j + 1 - c).astype(BF)
        psend[j, HD:, :] = part(dvt, 2 * j + 1 - c).astype(BF)
    send(psend, precv, dss.at[3], dsr.at[3], partner)
    got(precv, dsr.at[3])
    for off in range(1, NX):
        to = (y + off) % NX
        blk = 2 * to + c
        dsend[off - 1, :HD, :] = (part(dkt, blk) + precv[to, :HD, :].astype(F32)).astype(BF)
        dsend[off - 1, HD:, :] = (part(dvt, blk) + precv[to, HD:, :].astype(F32)).astype(BF)
        send(dsend.at[off - 1], drecv.at[off - 1], dss.at[off - 1], dsr.at[off - 1],
             dev(z, x, to, c))
    spread(NQ - 1)
    relay(0)

    dk = part(dkt, ctx) + precv[y, :HD, :].astype(F32)
    dv = part(dvt, ctx) + precv[y, HD:, :].astype(F32)
    for off in (1, 3, 2):
        got(drecv.at[off - 1], dsr.at[off - 1])
        dk = dk + drecv[off - 1, :HD, :].astype(F32)
        dv = dv + drecv[off - 1, HD:, :].astype(F32)
    dk = dk.T * F32(SCALE)
    bk_own[:, :HD] = (dk * cos_s[...] - pltpu.roll(dk, HD // 2, 1) * sin_s[...]).astype(BF)
    bk_own[:, HD:] = dv.T.astype(BF)
    spread(NQ)

    def across(step):
        return dev(z, (x + c * step) % NX, (y + (1 - c) * step) % NX, c)

    up_dev, down_dev = across(1), across(NX - 1)

    def term(a, ch):
        lhs = at[pl.ds(pl.multiple_of(a * 256, 256), 256), :]
        rhs = bq[ch] if ch < NQ else bk[...]
        return jnp.dot(lhs, rhs, preferred_element_type=F32)

    def stage(ch, s):
        cols = slice(STARTS[ch], STARTS[ch] + WIDTHS[ch])
        base = ch * 12
        if s == 0:
            y1s[:, cols] = term((opos + 2) % NX, ch).astype(BF)
            send(y1s.at[:128, cols], y1r.at[0, :, cols], cs.at[base], cr.at[base], up_dev)
            send(y1s.at[128:, cols], y1r.at[1, :, cols], cs.at[base + 1], cr.at[base + 1], down_dev)
        elif s == 1:
            t = term((opos + 1) % NX, ch)
            got(y1r.at[0, :, cols], cr.at[base])
            y2s[0, :128, cols] = (t[:128] + y1r[0, :, cols].astype(F32)).astype(BF)
            y2s[0, 128:, cols] = t[128:].astype(BF)
            send(y2s.at[0, :, cols], y2r.at[0, :, cols], cs.at[base + 2], cr.at[base + 2], up_dev)
            t = term((opos + NX - 1) % NX, ch)
            got(y1r.at[1, :, cols], cr.at[base + 1])
            y2s[1, :128, cols] = t[:128].astype(BF)
            y2s[1, 128:, cols] = (t[128:] + y1r[1, :, cols].astype(F32)).astype(BF)
            send(y2s.at[1, :, cols], y2r.at[1, :, cols], cs.at[base + 3], cr.at[base + 3], down_dev)
        elif s == 2:
            cacc[:, cols] = term(opos, ch)
            got(y2r.at[0, :, cols], cr.at[base + 2])
            got(y2r.at[1, :, cols], cr.at[base + 3])
            cacc[:, cols] += y2r[0, :, cols].astype(F32) + y2r[1, :, cols].astype(F32)
            for kind, dist, hop in ((0, 3, 1), (2, 4, 2), (1, 1, 1)):
                for d in range(2):
                    step, jump = (dist, hop) if d == 0 else (NZ - dist, NZ - hop)
                    row = pl.multiple_of(((z + step) % NZ) * 32, 32)
                    size = 32
                    if kind == 2:
                        row, size = row + 16 * d, 16
                    zs[d, kind, :size, cols] = cacc[pl.ds(row, size), cols].astype(BF)
                    sem = base + 4 + 2 * kind + d
                    send(zs.at[d, kind, :size, cols], zr.at[d, kind, :size, cols],
                         cs.at[sem], cr.at[sem], dev((z + jump) % NZ, x, y, c))
        elif s == 3:
            for d in range(2):
                hop = 2 if d == 0 else NZ - 2
                row = pl.multiple_of(((z + hop) % NZ) * 32, 32)
                got(zr.at[d, 0, :, cols], cr.at[base + 4 + d])
                low = cacc[pl.ds(row, 16), cols] + zr[d, 0, :16, cols].astype(F32)
                high = cacc[pl.ds(row + 16, 16), cols] + zr[d, 0, 16:, cols].astype(F32)
                got(zr.at[d, 2, :16, cols], cr.at[base + 8 + d])
                came = zr[d, 2, :16, cols].astype(F32)
                if d == 0:
                    low = low + came
                else:
                    high = high + came
                zs[d, 3, :16, cols] = low.astype(BF)
                zs[d, 3, 16:, cols] = high.astype(BF)
                send(zs.at[d, 3, :, cols], zr.at[d, 3, :, cols],
                     cs.at[base + 10 + d], cr.at[base + 10 + d], dev((z + hop) % NZ, x, y, c))
        else:
            total = cacc[pl.ds(pl.multiple_of(z * 32, 32), 32), cols]
            for kind in (1, 3):
                for d in range(2):
                    got(zr.at[d, kind, :, cols], cr.at[base + 4 + 2 * kind + d])
                    total = total + zr[d, kind, :, cols].astype(F32)
            out_ref[:, cols] = total

    for ch in range(1, NQ):
        relay(ch)
    own_a.wait()
    for k in range(7):
        got(at.at[:, mine], arcv.at[k])
    for t in range(5 + max(LAGS)):
        for ch in reversed(range(NCH)):
            s = t - LAGS[ch]
            if 0 <= s <= 4:
                if s == 0:
                    if ch == NQ:
                        relay(ch)
                    rest(ch)
                stage(ch, s)

    for copy in pending:
        copy.wait_send()


def body(tokens, qkv, grad_out, span_order):
    n_b = 7 * NCH
    n_c = 12 * NCH
    dma = pltpu.SemaphoreType.DMA
    v = pltpu.VMEM
    return pl.pallas_call(
        kernel,
        out_shape=jax.ShapeDtypeStruct((32, 1280), F32),
        in_specs=[pl.BlockSpec(memory_space=pl.ANY)] * 3
        + [pl.BlockSpec(memory_space=pltpu.SMEM)],
        out_specs=pl.BlockSpec(memory_space=pltpu.VMEM),
        scratch_shapes=[
            v((TDEV, 8192), BF), v((TDEV, 1280), BF), v((TDEV, QW), BF),
            v((SEQ, HD), BF), v((SEQ, HD), BF), v((SEQ, 2 * HD), BF),
            v((2 * TDEV, SEQ), F32), v((TDEV, HD), F32), v((TDEV, HD), F32),
            v((HD, SEQ), F32), v((HD, SEQ), F32),
            v((NX, 2 * HD, TDEV), BF), v((NX, 2 * HD, TDEV), BF),
            v((3, 2 * HD, TDEV), BF), v((3, 2 * HD, TDEV), BF),
            v((2, NX, 1024, TDEV), BF), v((1024, SEQ), BF),
            v((NQ, TDEV, QC), BF), v((TDEV, 256), BF), v((NQ, SEQ, QC), BF), v((SEQ, 256), BF),
            v((256, 1280), BF), v((2, 128, 1280), BF),
            v((2, 256, 1280), BF), v((2, 256, 1280), BF),
            v((256, 1280), F32), v((2, 4, 32, 1280), BF), v((2, 4, 32, 1280), BF),
            dma((4 + NCH,)), dma((7,)), dma((7,)), dma((7,)), dma((7,)), dma((4,)), dma((4,)),
            dma((n_b,)), dma((n_b,)), dma((n_c,)), dma((n_c,)),
        ],
        compiler_params=pltpu.CompilerParams(collective_id=0, has_side_effects=True),
    )(tokens, qkv, grad_out, span_order)


def solution(mesh):
    return jax.shard_map(
        body,
        mesh=mesh,
        in_specs=(
            P(("dp", "ctx"), None),
            P(("dp", "ctx"), None),
            P(("dp", "ctx"), None),
            P("dp", None),
        ),
        out_specs=P(("dp", "ctx"), None),
        check_vma=False,
    )
```

```python
import functools
import math

import jax
import jax.numpy as jnp
from jax import lax
from jax.experimental import pallas as pl
from jax.experimental.pallas import tpu as pltpu
from jax.sharding import PartitionSpec as P

HEADS = 8
HD = 128
TDEV = 128
SEQ = 1024
QW = HEADS * HD
NX = 4
NZ = 8
SPAN = 64
SPANS = 16
LOG_BASE = math.log(500000.0)
SCALE = 1.0 / math.sqrt(HD)
LOG2E = 1.4426950408889634
MESH = pl.DeviceIdType.MESH
BF = jnp.bfloat16
F32 = jnp.float32
NQ = 2
PER = HEADS // NQ
QC = QW // NQ
WIDTHS = (QC,) * NQ + (2 * HD,)
STARTS = tuple(QC * i for i in range(NQ)) + (QW,)
NCH = NQ + 1
GATHER_DIRECT = ()
FIRST_DIRECT = ()
Z_DIRECT = (2,)
FAR_AT = (0, 1)
ORDER = (
    "P", "S1", "R0", "D", "S2", "R1", "A", "G0", "F0", "R2", "G1", "F1", "N0",
    "G2", "F2", "N1", "Y0", "N2", "Y1", "Z0", "Y2", "Z1", "O0", "Z2", "O1", "O2",
)


def kernel(
    tok_h, qkv_h, go_h, span_s, out_ref,
    tokv, qkvv, gov, q_s, g_s, kv, bias, cos_s, sin_s, dkt, dvt, psend, precv, dsend, drecv,
    tr, at, bq_own, bk_own, bq, bk, y1s, y1r, y2s, y2r, cacc, zs, zr, zd,
    lsem, kvs, kvr, asnd, arcv, dss, dsr, bs, br, cs, cr,
):
    dp = lax.axis_index("dp")
    ctx = lax.axis_index("ctx")
    z = dp // NX
    x = dp % NX
    y = ctx // 2
    c = ctx % 2

    def dev(zz, xx, yy, cc):
        return (zz * NX + xx, yy * 2 + cc)

    def rcopy(src, dst, ssem, rsem, to):
        return pltpu.make_async_remote_copy(
            src_ref=src, dst_ref=dst, send_sem=ssem, recv_sem=rsem,
            device_id=to, device_id_type=MESH,
        )

    pending = []

    def send(src, dst, ssem, rsem, to):
        copy = rcopy(src, dst, ssem, rsem, to)
        copy.start()
        pending.append(copy)

    partner = dev(z, x, y, 1 - c)

    def got(dst, sem):
        rcopy(dst, dst, kvs.at[0], sem, partner).wait_recv()

    loads = [
        pltpu.make_async_copy(qkv_h, qkvv, lsem.at[0]),
        pltpu.make_async_copy(go_h, gov, lsem.at[1]),
        pltpu.make_async_copy(tok_h, tokv, lsem.at[2]),
    ]
    for load in loads:
        load.start()

    barrier = pltpu.get_barrier_semaphore()
    peers = [dev((z + off) % NZ, x, y, c) for off in ((1, 7, 2, 6, 3, 5, 4) if Z_DIRECT else (1, 7, 2, 6))]
    for off in range(1, NX):
        for cc in range(2):
            peers.append(dev(z, x, (y + off) % NX, cc))
            peers.append(dev(z, (x + off) % NX, y, cc))
    peers.append(partner)
    for peer in peers:
        pl.semaphore_signal(barrier, inc=1, device_id=peer, device_id_type=MESH)

    rows = lax.broadcasted_iota(jnp.int32, (TDEV, HD), 0)
    lanes = lax.broadcasted_iota(jnp.int32, (TDEV, HD), 1)
    first = span_s[0, 2 * ctx]
    second = span_s[0, 2 * ctx + 1]
    pos = jnp.where(rows < SPAN, first * SPAN + rows, second * SPAN + rows - SPAN)
    half = (lanes % (HD // 2)).astype(F32)
    freq = jnp.exp(half * (-2.0 / HD) * jnp.float32(LOG_BASE))
    angle = pos.astype(F32) * freq
    cosine = jnp.cos(angle)
    sine = jnp.sin(angle)
    sine = jnp.where(lanes < HD // 2, -sine, sine)
    cos_s[...] = cosine
    sin_s[...] = sine

    def rot(a):
        return a * cosine + pltpu.roll(a, HD // 2, 1) * sine

    loads[0].wait()
    kv_rows = pl.ds(pl.multiple_of(ctx * TDEV, TDEV), TDEV)
    kv[kv_rows, :HD] = rot(qkvv[:, QW:QW + HD].astype(F32)).astype(BF)
    kv[kv_rows, HD:] = qkvv[:, QW + HD:]

    loads[2].wait()

    def turn(zz, carry):
        for xx in range(NX):
            block = tokv[:, pl.ds(pl.multiple_of(zz * 1024 + xx * 256, 256), 256)]
            flip = block.T
            for yy in range(NX):
                at_row = pl.multiple_of(zz * 32, 32)
                tr[0, xx, pl.ds(yy * 256 + at_row, 32), :] = flip[yy * 64:yy * 64 + 32]
                tr[1, yy, pl.ds(xx * 256 + at_row, 32), :] = flip[yy * 64 + 32:yy * 64 + 64]
        return carry

    lax.fori_loop(0, NZ, turn, 0)

    for h in range(HEADS):
        q_s[h * TDEV:(h + 1) * TDEV, :] = rot(
            qkvv[:, h * HD:(h + 1) * HD].astype(F32)).astype(BF)
    loads[1].wait()
    for h in range(HEADS):
        g_s[h * TDEV:(h + 1) * TDEV, :] = gov[:, h * HD:(h + 1) * HD]
    key = lax.broadcasted_iota(jnp.int32, (1, SEQ), 1)
    key_span = key // SPAN
    key_pos = key % SPAN
    for i in range(SPANS):
        key_pos = key_pos + jnp.where(key_span == i, span_s[0, i] * SPAN, 0)
    masked = jnp.where(key_pos <= pos[:, :1], jnp.float32(0.0), jnp.float32(-1e30))
    bias[:TDEV, :] = masked
    bias[TDEV:, :] = masked
    dkt[...] = jnp.zeros_like(dkt)
    dvt[...] = jnp.zeros_like(dvt)

    pl.semaphore_wait(barrier, len(peers))

    own_kv = kv.at[kv_rows, :]
    for off in range(1, NX):
        send(own_kv, own_kv, kvs.at[off - 1], kvr.at[off - 1], dev(z, x, (y + off) % NX, c))
    send(own_kv, own_kv, kvs.at[3], kvr.at[3], partner)

    def slot(m):
        return pl.ds(pl.multiple_of(m * TDEV, TDEV), TDEV)

    gpos = x * (1 - c) + y * c
    opos = y * (1 - c) + x * c
    mine = slot(gpos * 2 + c)
    for off in (1, 3):
        to_x = (x + off) % NX
        to_y = (y + off) % NX
        send(tr.at[0, to_x], at.at[:, slot(x * 2 + c)],
             asnd.at[off - 1], arcv.at[(off - 1) * 2 + c], dev(z, to_x, y, 0))
        send(tr.at[1, to_y], at.at[:, slot(y * 2 + c)],
             asnd.at[off + 2], arcv.at[(off - 1) * 2 + c], dev(z, x, to_y, 1))

    def far_tokens(place):
        for n in range(2):
            if FAR_AT[n] == place:
                half = slice(512 * n, 512 * n + 512)
                to_x = (x + 2) % NX
                to_y = (y + 2) % NX
                send(tr.at[0, to_x, half], at.at[half, slot(x * 2 + c)],
                     asnd.at[1 + 6 * n], arcv.at[2 + 5 * n + c], dev(z, to_x, y, 0))
                send(tr.at[1, to_y, half], at.at[half, slot(y * 2 + c)],
                     asnd.at[4 + 4 * n], arcv.at[2 + 5 * n + c], dev(z, x, to_y, 1))

    send(tr.at[1 - c, opos], at.at[:, slot(opos * 2 + c)], asnd.at[6], arcv.at[6], partner)
    own_a = pltpu.make_async_copy(tr.at[c, gpos], at.at[:, mine], lsem.at[3])
    own_a.start()

    for off in (1, 3, 2):
        rows_in = slot(((y + NX - off) % NX) * 2 + c)
        got(kv.at[rows_in, :], kvr.at[off - 1])
        send(kv.at[rows_in, :], kv.at[rows_in, :], kvs.at[3 + off], kvr.at[3 + off], partner)
    got(own_kv, kvr.at[3])
    for off in (1, 3, 2):
        got(own_kv, kvr.at[3 + off])

    far_tokens(0)

    def heads(n, i, carry):
        pair = n * (PER // 2) + i
        two = pl.ds(pl.multiple_of(pair * 2 * TDEV, 2 * TDEV), 2 * TDEV)
        q2 = q_s[two, :]
        g2 = g_s[two, :]
        keys = kv[:, :HD]
        values = kv[:, HD:]
        s = lax.dot_general(q2, keys, (((1,), (1,)), ((), ())), preferred_element_type=F32)
        s = s * F32(SCALE * LOG2E) + bias[...]
        e = jnp.exp2(s - jnp.max(s, axis=1, keepdims=True))
        p = e * (1.0 / jnp.sum(e, axis=1, keepdims=True))
        pb = p.astype(BF)
        o = jnp.dot(pb, values, preferred_element_type=F32)
        delta = jnp.sum(g2.astype(F32) * o, axis=1, keepdims=True)
        dpr = lax.dot_general(g2, values, (((1,), (1,)), ((), ())), preferred_element_type=F32)
        ds = (p * (dpr - delta)).astype(BF)
        dq = jnp.dot(ds, keys, preferred_element_type=F32) * F32(SCALE)
        for j in range(2):
            g = dq[j * TDEV:(j + 1) * TDEV]
            back = g * cos_s[...] - pltpu.roll(g, HD // 2, 1) * sin_s[...]
            at_col = pl.multiple_of((2 * i + j) * HD, HD)
            bq_own[n, :, pl.ds(at_col, HD)] = back.astype(BF)
        dkt[...] += lax.dot_general(q2, ds, (((0,), (0,)), ((), ())), preferred_element_type=F32)
        dvt[...] += lax.dot_general(g2, pb, (((0,), (0,)), ((), ())), preferred_element_type=F32)
        return carry

    def own_of(ch):
        return bq_own.at[ch] if ch < NQ else bk_own

    def group_of(ch, where):
        return bq.at[ch, where, :] if ch < NQ else bk.at[where, :]

    local = []

    def spread(ch):
        own, base = own_of(ch), 7 * ch
        hops = (1, NX - 1, 2) if ch in GATHER_DIRECT else (1, NX - 1)
        for k, off in enumerate(hops):
            send(own, group_of(ch, slot(x * 2 + c)), bs.at[base + 2 * k],
                 br.at[base + 2 * k + c], dev(z, (x + off) % NX, y, 0))
            send(own, group_of(ch, slot(y * 2 + c)), bs.at[base + 2 * k + 1],
                 br.at[base + 2 * k + c], dev(z, x, (y + off) % NX, 1))
        send(own, group_of(ch, slot(opos * 2 + c)), bs.at[base + 6], br.at[base + 6], partner)
        copy = pltpu.make_async_copy(own, group_of(ch, mine), lsem.at[4 + ch])
        copy.start()
        local.append(copy)

    def beside(step):
        return dev(z, (x + (1 - c) * step) % NX, (y + c * step) % NX, c)

    below = (gpos + NX - 1) % NX
    above = (gpos + 1) % NX

    def relay(ch):
        if ch in GATHER_DIRECT:
            return
        base = 7 * ch
        up = group_of(ch, slot(below * 2))
        got(up, br.at[base])
        send(up, up, bs.at[base + 4], br.at[base + 4], beside(1))
        down = group_of(ch, slot(above * 2 + 1))
        got(down, br.at[base + 3])
        send(down, down, bs.at[base + 5], br.at[base + 5], beside(NX - 1))

    def rest(ch):
        local[ch].wait()
        for k in range(7) if ch in GATHER_DIRECT else (1, 2, 4, 5, 6):
            got(group_of(ch, mine), br.at[7 * ch + k])

    for n in range(NQ):
        lax.fori_loop(0, PER // 2, functools.partial(heads, n), 0)
        if n < NQ - 1:
            spread(n)
    far_tokens(1)

    def part(ref, blk):
        return ref[:, pl.ds(pl.multiple_of(blk * TDEV, TDEV), TDEV)]

    def chip_sum():
        for j in range(NX):
            psend[j, :HD, :] = part(dkt, 2 * j + 1 - c).astype(BF)
            psend[j, HD:, :] = part(dvt, 2 * j + 1 - c).astype(BF)
        send(psend, precv, dss.at[3], dsr.at[3], partner)
        got(precv, dsr.at[3])
        for off in range(1, NX):
            to = (y + off) % NX
            blk = 2 * to + c
            dsend[off - 1, :HD, :] = (part(dkt, blk) + precv[to, :HD, :].astype(F32)).astype(BF)
            dsend[off - 1, HD:, :] = (part(dvt, blk) + precv[to, HD:, :].astype(F32)).astype(BF)
            send(dsend.at[off - 1], drecv.at[off - 1], dss.at[off - 1], dsr.at[off - 1],
                 dev(z, x, to, c))

    def key_value_grads():
        dk = part(dkt, ctx) + precv[y, :HD, :].astype(F32)
        dv = part(dvt, ctx) + precv[y, HD:, :].astype(F32)
        for off in (1, 3, 2):
            got(drecv.at[off - 1], dsr.at[off - 1])
            dk = dk + drecv[off - 1, :HD, :].astype(F32)
            dv = dv + drecv[off - 1, HD:, :].astype(F32)
        dk = dk.T * F32(SCALE)
        bk_own[:, :HD] = (dk * cos_s[...] - pltpu.roll(dk, HD // 2, 1) * sin_s[...]).astype(BF)
        bk_own[:, HD:] = dv.T.astype(BF)

    def tokens_in():
        own_a.wait()
        for k in (0, 1, 4, 5, 6):
            got(at.at[:, mine], arcv.at[k])
        for k in (2, 3, 7, 8):
            got(at.at[:512, mine], arcv.at[k])


    def across(step):
        return dev(z, (x + c * step) % NX, (y + (1 - c) * step) % NX, c)

    up_dev, down_dev = across(1), across(NX - 1)

    def term(a, ch):
        lhs = at[pl.ds(pl.multiple_of(a * 256, 256), 256), :]
        rhs = bq[ch] if ch < NQ else bk[...]
        return jnp.dot(lhs, rhs, preferred_element_type=F32)

    def stage(ch, s):
        cols = slice(STARTS[ch], STARTS[ch] + WIDTHS[ch])
        base = ch * 12
        if s == 0 and ch in FIRST_DIRECT:
            for d, (blk, to) in enumerate(((opos + 1, up_dev), (opos + NX - 1, down_dev))):
                y2s[d, :, cols] = term(blk % NX, ch).astype(BF)
                send(y2s.at[d, :, cols], y2r.at[d, :, cols],
                     cs.at[base + 2 + d], cr.at[base + 2 + d], to)
            y1s[:, cols] = term((opos + 2) % NX, ch).astype(BF)
            for d in range(2):
                send(y1s.at[128 * d:128 * d + 128, cols], y1r.at[d, :, cols],
                     cs.at[base + d], cr.at[base + d], across(2))
        elif s == 1 and ch in FIRST_DIRECT:
            cacc[:, cols] = term(opos, ch)
        elif s == 0:
            y1s[:, cols] = term((opos + 2) % NX, ch).astype(BF)
            send(y1s.at[:128, cols], y1r.at[0, :, cols], cs.at[base], cr.at[base], up_dev)
            send(y1s.at[128:, cols], y1r.at[1, :, cols], cs.at[base + 1], cr.at[base + 1], down_dev)
        elif s == 1:
            t = term((opos + 1) % NX, ch)
            u = term((opos + NX - 1) % NX, ch)
            got(y1r.at[0, :, cols], cr.at[base])
            y2s[0, :128, cols] = (t[:128] + y1r[0, :, cols].astype(F32)).astype(BF)
            y2s[0, 128:, cols] = t[128:].astype(BF)
            send(y2s.at[0, :, cols], y2r.at[0, :, cols], cs.at[base + 2], cr.at[base + 2], up_dev)
            got(y1r.at[1, :, cols], cr.at[base + 1])
            y2s[1, :128, cols] = u[:128].astype(BF)
            y2s[1, 128:, cols] = (u[128:] + y1r[1, :, cols].astype(F32)).astype(BF)
            send(y2s.at[1, :, cols], y2r.at[1, :, cols], cs.at[base + 3], cr.at[base + 3], down_dev)
            cacc[:, cols] = term(opos, ch)
        elif s == 2:
            got(y2r.at[0, :, cols], cr.at[base + 2])
            got(y2r.at[1, :, cols], cr.at[base + 3])
            cacc[:, cols] += y2r[0, :, cols].astype(F32) + y2r[1, :, cols].astype(F32)
            if ch in FIRST_DIRECT:
                for d in range(2):
                    half = slice(128 * d, 128 * d + 128)
                    got(y1r.at[d, :, cols], cr.at[base + d])
                    cacc[half, cols] += y1r[d, :, cols].astype(F32)
            if ch in Z_DIRECT:
                for k, hop in enumerate((4, 3, 5, 2, 6, 1, 7)):
                    to = (z + hop) % NZ
                    row = pl.multiple_of(to * 32, 32)
                    zd[0, k, :, cols] = cacc[pl.ds(row, 32), cols].astype(BF)
                    send(zd.at[0, k, :, cols], zd.at[1, k, :, cols], cs.at[base + 4 + k], cr.at[base + 4 + k],
                         dev(to, x, y, c))
                return
            for kind, dist, hop in ((0, 3, 1), (2, 4, 2), (1, 1, 1)):
                for d in range(2):
                    step, jump = (dist, hop) if d == 0 else (NZ - dist, NZ - hop)
                    row = pl.multiple_of(((z + step) % NZ) * 32, 32)
                    size = 32
                    if kind == 2:
                        row, size = row + 16 * d, 16
                    zs[d, kind, :size, cols] = cacc[pl.ds(row, size), cols].astype(BF)
                    sem = base + 4 + 2 * kind + d
                    send(zs.at[d, kind, :size, cols], zr.at[d, kind, :size, cols],
                         cs.at[sem], cr.at[sem], dev((z + jump) % NZ, x, y, c))
        elif s == 3 and ch in Z_DIRECT:
            pass
        elif s == 4 and ch in Z_DIRECT:
            total = cacc[pl.ds(pl.multiple_of(z * 32, 32), 32), cols]
            for k in range(7):
                got(zd.at[1, k, :, cols], cr.at[base + 4 + k])
                total = total + zd[1, k, :, cols].astype(F32)
            out_ref[:, cols] = total
        elif s == 3:
            for d in range(2):
                hop = 2 if d == 0 else NZ - 2
                row = pl.multiple_of(((z + hop) % NZ) * 32, 32)
                got(zr.at[d, 0, :, cols], cr.at[base + 4 + d])
                low = cacc[pl.ds(row, 16), cols] + zr[d, 0, :16, cols].astype(F32)
                high = cacc[pl.ds(row + 16, 16), cols] + zr[d, 0, 16:, cols].astype(F32)
                got(zr.at[d, 2, :16, cols], cr.at[base + 8 + d])
                came = zr[d, 2, :16, cols].astype(F32)
                if d == 0:
                    low = low + came
                else:
                    high = high + came
                zs[d, 3, :16, cols] = low.astype(BF)
                zs[d, 3, 16:, cols] = high.astype(BF)
                send(zs.at[d, 3, :, cols], zr.at[d, 3, :, cols],
                     cs.at[base + 10 + d], cr.at[base + 10 + d], dev((z + hop) % NZ, x, y, c))
        else:
            total = cacc[pl.ds(pl.multiple_of(z * 32, 32), 32), cols]
            for kind in (1, 3):
                for d in range(2):
                    got(zr.at[d, kind, :, cols], cr.at[base + 4 + 2 * kind + d])
                    total = total + zr[d, kind, :, cols].astype(F32)
            out_ref[:, cols] = total

    for op in ORDER:
        ch = int(op[1:] or 0)
        if op == "P":
            chip_sum()
        elif op == "D":
            key_value_grads()
        elif op == "A":
            tokens_in()
        elif op[0] in "SRG":
            {"S": spread, "R": relay, "G": rest}[op[0]](ch)
        else:
            stage(ch, "FNYZO".index(op[0]))

    for copy in pending:
        copy.wait_send()


def body(tokens, qkv, grad_out, span_order):
    n_b = 7 * NCH
    n_c = 12 * NCH
    dma = pltpu.SemaphoreType.DMA
    v = pltpu.VMEM
    return pl.pallas_call(
        kernel,
        out_shape=jax.ShapeDtypeStruct((32, 1280), F32),
        in_specs=[pl.BlockSpec(memory_space=pl.ANY)] * 3
        + [pl.BlockSpec(memory_space=pltpu.SMEM)],
        out_specs=pl.BlockSpec(memory_space=pltpu.VMEM),
        scratch_shapes=[
            v((TDEV, 8192), BF), v((TDEV, 1280), BF), v((TDEV, QW), BF),
            v((SEQ, HD), BF), v((SEQ, HD), BF), v((SEQ, 2 * HD), BF),
            v((2 * TDEV, SEQ), F32), v((TDEV, HD), F32), v((TDEV, HD), F32),
            v((HD, SEQ), F32), v((HD, SEQ), F32),
            v((NX, 2 * HD, TDEV), BF), v((NX, 2 * HD, TDEV), BF),
            v((3, 2 * HD, TDEV), BF), v((3, 2 * HD, TDEV), BF),
            v((2, NX, 1024, TDEV), BF), v((1024, SEQ), BF),
            v((NQ, TDEV, QC), BF), v((TDEV, 256), BF), v((NQ, SEQ, QC), BF), v((SEQ, 256), BF),
            v((256, 1280), BF), v((2, 128, 1280), BF),
            v((2, 256, 1280), BF), v((2, 256, 1280), BF),
            v((256, 1280), F32), v((2, 4, 32, 1280), BF), v((2, 4, 32, 1280), BF), v((2, 7, 32, 1280), BF),
            dma((4 + NCH,)), dma((7,)), dma((7,)), dma((9,)), dma((9,)), dma((4,)), dma((4,)),
            dma((n_b,)), dma((n_b,)), dma((n_c,)), dma((n_c,)),
        ],
        compiler_params=pltpu.CompilerParams(collective_id=0, has_side_effects=True),
    )(tokens, qkv, grad_out, span_order)


def solution(mesh):
    return jax.shard_map(
        body,
        mesh=mesh,
        in_specs=(
            P(("dp", "ctx"), None),
            P(("dp", "ctx"), None),
            P(("dp", "ctx"), None),
            P("dp", None),
        ),
        out_specs=P(("dp", "ctx"), None),
        check_vma=False,
    )
```

```python
import functools
import math

import jax
import jax.numpy as jnp
from jax import lax
from jax.experimental import pallas as pl
from jax.experimental.pallas import tpu as pltpu
from jax.sharding import PartitionSpec as P

HEADS = 8
HD = 128
TDEV = 128
SEQ = 1024
QW = HEADS * HD
NX = 4
NZ = 8
SPAN = 64
SPANS = 16
LOG_BASE = math.log(500000.0)
SCALE = 1.0 / math.sqrt(HD)
LOG2E = 1.4426950408889634
MESH = pl.DeviceIdType.MESH
BF = jnp.bfloat16
F32 = jnp.float32
NQ = 2
PER = HEADS // NQ
QC = QW // NQ
WIDTHS = (QC,) * NQ + (2 * HD,)
STARTS = tuple(QC * i for i in range(NQ)) + (QW,)
NCH = NQ + 1
GATHER_DIRECT = ()
FIRST_DIRECT = ()
Z_DIRECT = (0, 2)
FAR_AT = (0, 1)
ORDER = (
    "P", "S1", "R0", "D", "S2", "R1", "A", "G0", "F0", "R2", "G1", "F1", "N0",
    "G2", "F2", "N1", "Y0", "N2", "Y1", "Z0", "Y2", "Z1", "O0", "Z2", "O1", "O2",
)


def kernel(
    tok_h, qkv_h, go_h, span_s, out_ref,
    tokv, qkvv, gov, q_s, g_s, kv, bias, cos_s, sin_s, dkt, dvt, psend, precv, dsend, drecv,
    tr, at, bq_own, bk_own, bq, bk, y1s, y1r, y2s, y2r, cacc, zs, zr, zd,
    lsem, kvs, kvr, asnd, arcv, dss, dsr, bs, br, cs, cr,
):
    dp = lax.axis_index("dp")
    ctx = lax.axis_index("ctx")
    z = dp // NX
    x = dp % NX
    y = ctx // 2
    c = ctx % 2

    def dev(zz, xx, yy, cc):
        return (zz * NX + xx, yy * 2 + cc)

    def rcopy(src, dst, ssem, rsem, to):
        return pltpu.make_async_remote_copy(
            src_ref=src, dst_ref=dst, send_sem=ssem, recv_sem=rsem,
            device_id=to, device_id_type=MESH,
        )

    pending = []

    def send(src, dst, ssem, rsem, to):
        copy = rcopy(src, dst, ssem, rsem, to)
        copy.start()
        pending.append(copy)

    partner = dev(z, x, y, 1 - c)

    def got(dst, sem):
        rcopy(dst, dst, kvs.at[0], sem, partner).wait_recv()

    loads = [
        pltpu.make_async_copy(qkv_h, qkvv, lsem.at[0]),
        pltpu.make_async_copy(go_h, gov, lsem.at[1]),
        pltpu.make_async_copy(tok_h, tokv, lsem.at[2]),
    ]
    for load in loads:
        load.start()

    barrier = pltpu.get_barrier_semaphore()
    peers = [dev((z + off) % NZ, x, y, c) for off in ((1, 7, 2, 6, 3, 5, 4) if Z_DIRECT else (1, 7, 2, 6))]
    for off in range(1, NX):
        for cc in range(2):
            peers.append(dev(z, x, (y + off) % NX, cc))
            peers.append(dev(z, (x + off) % NX, y, cc))
    peers.append(partner)
    for peer in peers:
        pl.semaphore_signal(barrier, inc=1, device_id=peer, device_id_type=MESH)

    rows = lax.broadcasted_iota(jnp.int32, (TDEV, HD), 0)
    lanes = lax.broadcasted_iota(jnp.int32, (TDEV, HD), 1)
    first = span_s[0, 2 * ctx]
    second = span_s[0, 2 * ctx + 1]
    pos = jnp.where(rows < SPAN, first * SPAN + rows, second * SPAN + rows - SPAN)
    half = (lanes % (HD // 2)).astype(F32)
    freq = jnp.exp(half * (-2.0 / HD) * jnp.float32(LOG_BASE))
    angle = pos.astype(F32) * freq
    cosine = jnp.cos(angle)
    sine = jnp.sin(angle)
    sine = jnp.where(lanes < HD // 2, -sine, sine)
    cos_s[...] = cosine
    sin_s[...] = sine

    def rot(a):
        return a * cosine + pltpu.roll(a, HD // 2, 1) * sine

    loads[0].wait()
    kv_rows = pl.ds(pl.multiple_of(ctx * TDEV, TDEV), TDEV)
    kv[kv_rows, :HD] = rot(qkvv[:, QW:QW + HD].astype(F32)).astype(BF)
    kv[kv_rows, HD:] = qkvv[:, QW + HD:]

    loads[2].wait()

    def turn(zz, carry):
        for xx in range(NX):
            block = tokv[:, pl.ds(pl.multiple_of(zz * 1024 + xx * 256, 256), 256)]
            flip = block.T
            for yy in range(NX):
                at_row = pl.multiple_of(zz * 32, 32)
                tr[0, xx, pl.ds(yy * 256 + at_row, 32), :] = flip[yy * 64:yy * 64 + 32]
                tr[1, yy, pl.ds(xx * 256 + at_row, 32), :] = flip[yy * 64 + 32:yy * 64 + 64]
        return carry

    lax.fori_loop(0, NZ, turn, 0)

    for h in range(HEADS):
        q_s[h * TDEV:(h + 1) * TDEV, :] = rot(
            qkvv[:, h * HD:(h + 1) * HD].astype(F32)).astype(BF)
    loads[1].wait()
    for h in range(HEADS):
        g_s[h * TDEV:(h + 1) * TDEV, :] = gov[:, h * HD:(h + 1) * HD]
    key = lax.broadcasted_iota(jnp.int32, (1, SEQ), 1)
    key_span = key // SPAN
    key_pos = key % SPAN
    for i in range(SPANS):
        key_pos = key_pos + jnp.where(key_span == i, span_s[0, i] * SPAN, 0)
    masked = jnp.where(key_pos <= pos[:, :1], jnp.float32(0.0), jnp.float32(-1e30))
    bias[:TDEV, :] = masked
    bias[TDEV:, :] = masked
    dkt[...] = jnp.zeros_like(dkt)
    dvt[...] = jnp.zeros_like(dvt)

    pl.semaphore_wait(barrier, len(peers))

    own_kv = kv.at[kv_rows, :]
    for off in range(1, NX):
        send(own_kv, own_kv, kvs.at[off - 1], kvr.at[off - 1], dev(z, x, (y + off) % NX, c))
    send(own_kv, own_kv, kvs.at[3], kvr.at[3], partner)

    def slot(m):
        return pl.ds(pl.multiple_of(m * TDEV, TDEV), TDEV)

    gpos = x * (1 - c) + y * c
    opos = y * (1 - c) + x * c
    mine = slot(gpos * 2 + c)
    for off in (1, 3):
        to_x = (x + off) % NX
        to_y = (y + off) % NX
        send(tr.at[0, to_x], at.at[:, slot(x * 2 + c)],
             asnd.at[off - 1], arcv.at[(off - 1) * 2 + c], dev(z, to_x, y, 0))
        send(tr.at[1, to_y], at.at[:, slot(y * 2 + c)],
             asnd.at[off + 2], arcv.at[(off - 1) * 2 + c], dev(z, x, to_y, 1))

    def far_tokens(place):
        for n in range(2):
            if FAR_AT[n] == place:
                half = slice(512 * n, 512 * n + 512)
                to_x = (x + 2) % NX
                to_y = (y + 2) % NX
                send(tr.at[0, to_x, half], at.at[half, slot(x * 2 + c)],
                     asnd.at[1 + 6 * n], arcv.at[2 + 5 * n + c], dev(z, to_x, y, 0))
                send(tr.at[1, to_y, half], at.at[half, slot(y * 2 + c)],
                     asnd.at[4 + 4 * n], arcv.at[2 + 5 * n + c], dev(z, x, to_y, 1))

    send(tr.at[1 - c, opos], at.at[:, slot(opos * 2 + c)], asnd.at[6], arcv.at[6], partner)
    own_a = pltpu.make_async_copy(tr.at[c, gpos], at.at[:, mine], lsem.at[3])
    own_a.start()

    for off in (1, 3, 2):
        rows_in = slot(((y + NX - off) % NX) * 2 + c)
        got(kv.at[rows_in, :], kvr.at[off - 1])
        send(kv.at[rows_in, :], kv.at[rows_in, :], kvs.at[3 + off], kvr.at[3 + off], partner)
    got(own_kv, kvr.at[3])
    for off in (1, 3, 2):
        got(own_kv, kvr.at[3 + off])

    far_tokens(0)

    def heads(n, i, carry):
        pair = n * (PER // 2) + i
        two = pl.ds(pl.multiple_of(pair * 2 * TDEV, 2 * TDEV), 2 * TDEV)
        q2 = q_s[two, :]
        g2 = g_s[two, :]
        keys = kv[:, :HD]
        values = kv[:, HD:]
        s = lax.dot_general(q2, keys, (((1,), (1,)), ((), ())), preferred_element_type=F32)
        s = s * F32(SCALE * LOG2E) + bias[...]
        e = jnp.exp2(s - jnp.max(s, axis=1, keepdims=True))
        p = e * (1.0 / jnp.sum(e, axis=1, keepdims=True))
        pb = p.astype(BF)
        o = jnp.dot(pb, values, preferred_element_type=F32)
        delta = jnp.sum(g2.astype(F32) * o, axis=1, keepdims=True)
        dpr = lax.dot_general(g2, values, (((1,), (1,)), ((), ())), preferred_element_type=F32)
        ds = (p * (dpr - delta)).astype(BF)
        dq = jnp.dot(ds, keys, preferred_element_type=F32) * F32(SCALE)
        for j in range(2):
            g = dq[j * TDEV:(j + 1) * TDEV]
            back = g * cos_s[...] - pltpu.roll(g, HD // 2, 1) * sin_s[...]
            at_col = pl.multiple_of((2 * i + j) * HD, HD)
            bq_own[n, :, pl.ds(at_col, HD)] = back.astype(BF)
        dkt[...] += lax.dot_general(q2, ds, (((0,), (0,)), ((), ())), preferred_element_type=F32)
        dvt[...] += lax.dot_general(g2, pb, (((0,), (0,)), ((), ())), preferred_element_type=F32)
        return carry

    def own_of(ch):
        return bq_own.at[ch] if ch < NQ else bk_own

    def group_of(ch, where):
        return bq.at[ch, where, :] if ch < NQ else bk.at[where, :]

    local = []

    def spread(ch):
        own, base = own_of(ch), 7 * ch
        hops = (1, NX - 1, 2) if ch in GATHER_DIRECT else (1, NX - 1)
        for k, off in enumerate(hops):
            send(own, group_of(ch, slot(x * 2 + c)), bs.at[base + 2 * k],
                 br.at[base + 2 * k + c], dev(z, (x + off) % NX, y, 0))
            send(own, group_of(ch, slot(y * 2 + c)), bs.at[base + 2 * k + 1],
                 br.at[base + 2 * k + c], dev(z, x, (y + off) % NX, 1))
        send(own, group_of(ch, slot(opos * 2 + c)), bs.at[base + 6], br.at[base + 6], partner)
        copy = pltpu.make_async_copy(own, group_of(ch, mine), lsem.at[4 + ch])
        copy.start()
        local.append(copy)

    def beside(step):
        return dev(z, (x + (1 - c) * step) % NX, (y + c * step) % NX, c)

    below = (gpos + NX - 1) % NX
    above = (gpos + 1) % NX

    def relay(ch):
        if ch in GATHER_DIRECT:
            return
        base = 7 * ch
        up = group_of(ch, slot(below * 2))
        got(up, br.at[base])
        send(up, up, bs.at[base + 4], br.at[base + 4], beside(1))
        down = group_of(ch, slot(above * 2 + 1))
        got(down, br.at[base + 3])
        send(down, down, bs.at[base + 5], br.at[base + 5], beside(NX - 1))

    def rest(ch):
        local[ch].wait()
        for k in range(7) if ch in GATHER_DIRECT else (1, 2, 4, 5, 6):
            got(group_of(ch, mine), br.at[7 * ch + k])

    for n in range(NQ):
        lax.fori_loop(0, PER // 2, functools.partial(heads, n), 0)
        if n < NQ - 1:
            spread(n)
    far_tokens(1)

    def part(ref, blk):
        return ref[:, pl.ds(pl.multiple_of(blk * TDEV, TDEV), TDEV)]

    def chip_sum():
        for j in range(NX):
            psend[j, :HD, :] = part(dkt, 2 * j + 1 - c).astype(BF)
            psend[j, HD:, :] = part(dvt, 2 * j + 1 - c).astype(BF)
        send(psend, precv, dss.at[3], dsr.at[3], partner)
        got(precv, dsr.at[3])
        for off in range(1, NX):
            to = (y + off) % NX
            blk = 2 * to + c
            dsend[off - 1, :HD, :] = (part(dkt, blk) + precv[to, :HD, :].astype(F32)).astype(BF)
            dsend[off - 1, HD:, :] = (part(dvt, blk) + precv[to, HD:, :].astype(F32)).astype(BF)
            send(dsend.at[off - 1], drecv.at[off - 1], dss.at[off - 1], dsr.at[off - 1],
                 dev(z, x, to, c))

    def key_value_grads():
        dk = part(dkt, ctx) + precv[y, :HD, :].astype(F32)
        dv = part(dvt, ctx) + precv[y, HD:, :].astype(F32)
        for off in (1, 3, 2):
            got(drecv.at[off - 1], dsr.at[off - 1])
            dk = dk + drecv[off - 1, :HD, :].astype(F32)
            dv = dv + drecv[off - 1, HD:, :].astype(F32)
        dk = dk.T * F32(SCALE)
        bk_own[:, :HD] = (dk * cos_s[...] - pltpu.roll(dk, HD // 2, 1) * sin_s[...]).astype(BF)
        bk_own[:, HD:] = dv.T.astype(BF)

    def tokens_in():
        own_a.wait()
        for k in (0, 1, 4, 5, 6):
            got(at.at[:, mine], arcv.at[k])
        for k in (2, 3, 7, 8):
            got(at.at[:512, mine], arcv.at[k])


    def across(step):
        return dev(z, (x + c * step) % NX, (y + (1 - c) * step) % NX, c)

    up_dev, down_dev = across(1), across(NX - 1)

    def term(a, ch):
        lhs = at[pl.ds(pl.multiple_of(a * 256, 256), 256), :]
        rhs = bq[ch] if ch < NQ else bk[...]
        return jnp.dot(lhs, rhs, preferred_element_type=F32)

    def stage(ch, s):
        cols = slice(STARTS[ch], STARTS[ch] + WIDTHS[ch])
        base = ch * 12
        if s == 0 and ch in FIRST_DIRECT:
            for d, (blk, to) in enumerate(((opos + 1, up_dev), (opos + NX - 1, down_dev))):
                y2s[d, :, cols] = term(blk % NX, ch).astype(BF)
                send(y2s.at[d, :, cols], y2r.at[d, :, cols],
                     cs.at[base + 2 + d], cr.at[base + 2 + d], to)
            y1s[:, cols] = term((opos + 2) % NX, ch).astype(BF)
            for d in range(2):
                send(y1s.at[128 * d:128 * d + 128, cols], y1r.at[d, :, cols],
                     cs.at[base + d], cr.at[base + d], across(2))
        elif s == 1 and ch in FIRST_DIRECT:
            cacc[:, cols] = term(opos, ch)
        elif s == 0:
            y1s[:, cols] = term((opos + 2) % NX, ch).astype(BF)
            send(y1s.at[:128, cols], y1r.at[0, :, cols], cs.at[base], cr.at[base], up_dev)
            send(y1s.at[128:, cols], y1r.at[1, :, cols], cs.at[base + 1], cr.at[base + 1], down_dev)
        elif s == 1:
            t = term((opos + 1) % NX, ch)
            u = term((opos + NX - 1) % NX, ch)
            got(y1r.at[0, :, cols], cr.at[base])
            y2s[0, :128, cols] = (t[:128] + y1r[0, :, cols].astype(F32)).astype(BF)
            y2s[0, 128:, cols] = t[128:].astype(BF)
            send(y2s.at[0, :, cols], y2r.at[0, :, cols], cs.at[base + 2], cr.at[base + 2], up_dev)
            got(y1r.at[1, :, cols], cr.at[base + 1])
            y2s[1, :128, cols] = u[:128].astype(BF)
            y2s[1, 128:, cols] = (u[128:] + y1r[1, :, cols].astype(F32)).astype(BF)
            send(y2s.at[1, :, cols], y2r.at[1, :, cols], cs.at[base + 3], cr.at[base + 3], down_dev)
            cacc[:, cols] = term(opos, ch)
        elif s == 2:
            got(y2r.at[0, :, cols], cr.at[base + 2])
            got(y2r.at[1, :, cols], cr.at[base + 3])
            cacc[:, cols] += y2r[0, :, cols].astype(F32) + y2r[1, :, cols].astype(F32)
            if ch in FIRST_DIRECT:
                for d in range(2):
                    half = slice(128 * d, 128 * d + 128)
                    got(y1r.at[d, :, cols], cr.at[base + d])
                    cacc[half, cols] += y1r[d, :, cols].astype(F32)
            if ch in Z_DIRECT:
                for k, hop in enumerate((4, 3, 5, 2, 6, 1, 7)):
                    to = (z + hop) % NZ
                    row = pl.multiple_of(to * 32, 32)
                    zd[0, k, :, cols] = cacc[pl.ds(row, 32), cols].astype(BF)
                    send(zd.at[0, k, :, cols], zd.at[1, k, :, cols], cs.at[base + 4 + k], cr.at[base + 4 + k],
                         dev(to, x, y, c))
                return
            for kind, dist, hop in ((0, 3, 1), (2, 4, 2), (1, 1, 1)):
                for d in range(2):
                    step, jump = (dist, hop) if d == 0 else (NZ - dist, NZ - hop)
                    row = pl.multiple_of(((z + step) % NZ) * 32, 32)
                    size = 32
                    if kind == 2:
                        row, size = row + 16 * d, 16
                    zs[d, kind, :size, cols] = cacc[pl.ds(row, size), cols].astype(BF)
                    sem = base + 4 + 2 * kind + d
                    send(zs.at[d, kind, :size, cols], zr.at[d, kind, :size, cols],
                         cs.at[sem], cr.at[sem], dev((z + jump) % NZ, x, y, c))
        elif s == 3 and ch in Z_DIRECT:
            pass
        elif s == 4 and ch in Z_DIRECT:
            total = cacc[pl.ds(pl.multiple_of(z * 32, 32), 32), cols]
            for k in range(7):
                got(zd.at[1, k, :, cols], cr.at[base + 4 + k])
                total = total + zd[1, k, :, cols].astype(F32)
            out_ref[:, cols] = total
        elif s == 3:
            for d in range(2):
                hop = 2 if d == 0 else NZ - 2
                row = pl.multiple_of(((z + hop) % NZ) * 32, 32)
                got(zr.at[d, 0, :, cols], cr.at[base + 4 + d])
                low = cacc[pl.ds(row, 16), cols] + zr[d, 0, :16, cols].astype(F32)
                high = cacc[pl.ds(row + 16, 16), cols] + zr[d, 0, 16:, cols].astype(F32)
                got(zr.at[d, 2, :16, cols], cr.at[base + 8 + d])
                came = zr[d, 2, :16, cols].astype(F32)
                if d == 0:
                    low = low + came
                else:
                    high = high + came
                zs[d, 3, :16, cols] = low.astype(BF)
                zs[d, 3, 16:, cols] = high.astype(BF)
                send(zs.at[d, 3, :, cols], zr.at[d, 3, :, cols],
                     cs.at[base + 10 + d], cr.at[base + 10 + d], dev((z + hop) % NZ, x, y, c))
        else:
            total = cacc[pl.ds(pl.multiple_of(z * 32, 32), 32), cols]
            for kind in (1, 3):
                for d in range(2):
                    got(zr.at[d, kind, :, cols], cr.at[base + 4 + 2 * kind + d])
                    total = total + zr[d, kind, :, cols].astype(F32)
            out_ref[:, cols] = total

    for op in ORDER:
        ch = int(op[1:] or 0)
        if op == "P":
            chip_sum()
        elif op == "D":
            key_value_grads()
        elif op == "A":
            tokens_in()
        elif op[0] in "SRG":
            {"S": spread, "R": relay, "G": rest}[op[0]](ch)
        else:
            stage(ch, "FNYZO".index(op[0]))

    for copy in pending:
        copy.wait_send()


def body(tokens, qkv, grad_out, span_order):
    n_b = 7 * NCH
    n_c = 12 * NCH
    dma = pltpu.SemaphoreType.DMA
    v = pltpu.VMEM
    return pl.pallas_call(
        kernel,
        out_shape=jax.ShapeDtypeStruct((32, 1280), F32),
        in_specs=[pl.BlockSpec(memory_space=pl.ANY)] * 3
        + [pl.BlockSpec(memory_space=pltpu.SMEM)],
        out_specs=pl.BlockSpec(memory_space=pltpu.VMEM),
        scratch_shapes=[
            v((TDEV, 8192), BF), v((TDEV, 1280), BF), v((TDEV, QW), BF),
            v((SEQ, HD), BF), v((SEQ, HD), BF), v((SEQ, 2 * HD), BF),
            v((2 * TDEV, SEQ), F32), v((TDEV, HD), F32), v((TDEV, HD), F32),
            v((HD, SEQ), F32), v((HD, SEQ), F32),
            v((NX, 2 * HD, TDEV), BF), v((NX, 2 * HD, TDEV), BF),
            v((3, 2 * HD, TDEV), BF), v((3, 2 * HD, TDEV), BF),
            v((2, NX, 1024, TDEV), BF), v((1024, SEQ), BF),
            v((NQ, TDEV, QC), BF), v((TDEV, 256), BF), v((NQ, SEQ, QC), BF), v((SEQ, 256), BF),
            v((256, 1280), BF), v((2, 128, 1280), BF),
            v((2, 256, 1280), BF), v((2, 256, 1280), BF),
            v((256, 1280), F32), v((2, 4, 32, 1280), BF), v((2, 4, 32, 1280), BF), v((2, 7, 32, 1280), BF),
            dma((4 + NCH,)), dma((7,)), dma((7,)), dma((9,)), dma((9,)), dma((4,)), dma((4,)),
            dma((n_b,)), dma((n_b,)), dma((n_c,)), dma((n_c,)),
        ],
        compiler_params=pltpu.CompilerParams(collective_id=0, has_side_effects=True),
    )(tokens, qkv, grad_out, span_order)


def solution(mesh):
    return jax.shard_map(
        body,
        mesh=mesh,
        in_specs=(
            P(("dp", "ctx"), None),
            P(("dp", "ctx"), None),
            P(("dp", "ctx"), None),
            P("dp", None),
        ),
        out_specs=P(("dp", "ctx"), None),
        check_vma=False,
    )
```
